32 devices in a mesh: ctx: 8 (over z, core), head: 4 (over y, x).
Axes of the slice: x: 2, y: 2, z: 4, core: 2. Of those that a mesh axis runs over, the one named last changes fastest.
Arguments:
- query: bfloat16 [4096, 64, 128], P('ctx', 'head'), may hold values from -8 to 8
- keys: bfloat16 [4096, 8, 128], P('ctx', 'head'), may hold values from -8 to 8
- values: bfloat16 [4096, 8, 128], P('ctx', 'head'), may hold values from -6 to 6
- k_scale: bfloat16 [16, 8], P('ctx', 'head'), may hold values from 0.59765625 to 1.59375
- v_scale: bfloat16 [16, 8], P('ctx', 'head'), may hold values from 0.5 to 2
- block_place: int32 [16], P('ctx'), may hold values from 0 to 15, as said below
- out_weight: bfloat16 [8192, 8192], P('head'), may hold values from -1 to 1
Outputs:
- mixed: bfloat16 [4096, 8192], P(('ctx', 'head'))
The draws below stay inside these ranges and needn't reach their ends.
Inputs may be any that keep to these rules, and one draw needn't show every extreme that they name: `block_place`: A permutation of the block indices in which entries 2r and 2r + 1 sum to 15 and entry 2r is below 8.
All inputs are finite; a program needn't handle non-finite values.
Results may differ from the reference program's by a relative error of at most 0.015.
Values may be sent and summed in bfloat16 or wider, within the bound.
A program may use at most 128 MiB of HBM per device.

```python
import math
import jax
import jax.numpy as jnp
from jax import lax

HQ = 64
KVH = 8
DH = 128
D = 8192
BLK = 256
NBLOCK = 16
TOKENS = 4096
HEAD_DEV = 16
N_HEAD = 4


def draw_query(key, part):
    shape = (TOKENS, HQ, DH)
    result = jnp.clip(jax.random.normal(jax.random.fold_in(key, 1), shape, jnp.float32), -6.0, 6.0)
    return result.astype(jnp.bfloat16)


def draw_keys(key, part):
    shape = (TOKENS, KVH, DH)
    result = jnp.clip(jax.random.normal(jax.random.fold_in(key, 2), shape, jnp.float32), -6.0, 6.0)
    return result.astype(jnp.bfloat16)


def draw_block_place(key, part):
    shuffled = jax.random.permutation(jax.random.fold_in(key, 3), NBLOCK // 2).astype(jnp.int32)
    return jnp.stack([shuffled, NBLOCK - 1 - shuffled], axis=1).reshape(NBLOCK).astype(jnp.int32)


def block_scale(rng, shape, pieces, smallest, high):
    level, own = 1.0, jax.random.fold_in(rng, 6)
    for dim, blocks in pieces:
        draws = jnp.exp(jax.random.uniform(jax.random.fold_in(own, dim), (blocks,), jnp.float32, smallest / len(pieces), high / len(pieces)))
        level = level * jnp.repeat(draws, shape[dim] // blocks).reshape([-1 if axis == dim else 1 for axis in range(len(shape))])
    return level


def normal_values(stream_key, extent, spread, most, cuts=(), held_as=jnp.bfloat16):
    values = jax.random.normal(stream_key, extent, jnp.float32) * spread
    if len(cuts) > 0:
        values = block_scale(stream_key, extent, cuts, -0.22, 0.18) * values
    return jnp.clip(values, min=-most, max=most).astype(held_as)


def setup_inputs(seed: int = 0) -> dict:
    splits = jax.random.split(jax.random.key(seed), 8)
    query = draw_query(jax.random.fold_in(splits[7], 71), 0)
    keys = draw_keys(jax.random.fold_in(splits[7], 71), 0)
    values = normal_values(splits[2], (TOKENS, KVH, DH), 1.0, 6.0, ((0, 8), (1, 4)))
    k_scale = jnp.clip(jnp.exp(math.log(1.59375) - 0.98082925 * jax.random.uniform(splits[3], (NBLOCK, KVH), jnp.float32) ** block_scale(splits[3], (NBLOCK, KVH), ((0, 8), (1, 4)), -0.2, 0.2)), 0.59765625, 1.59375).astype(jnp.bfloat16)
    v_scale = jnp.clip(jnp.exp(math.log(2.0) - 1.3862944 * jax.random.uniform(splits[4], (NBLOCK, KVH), jnp.float32) ** block_scale(splits[4], (NBLOCK, KVH), ((0, 8), (1, 4)), -0.2, 0.2)), 0.5, 2.0).astype(jnp.bfloat16)
    block_place = draw_block_place(jax.random.fold_in(splits[7], 71), 0)
    out_weight = normal_values(splits[6], (HQ * DH, D), (HQ * DH // 256) ** -0.5, 1.0, ((0, 4),))
    return {"query": query, "keys": keys, "values": values, "k_scale": k_scale, "v_scale": v_scale, "block_place": block_place, "out_weight": out_weight}


masked_value = -1e+30

def reference(query, keys, values, k_scale, v_scale, block_place, out_weight):
    group_size = HQ // KVH
    inv_root = 1.0 / math.sqrt(DH)
    token_place = (block_place[:, None] * BLK + jnp.arange(BLK, dtype=jnp.int32)[None, :]).reshape(TOKENS).astype(jnp.int32)
    key_gain = jnp.repeat(k_scale.astype(jnp.float32), BLK, axis=0)
    value_gain = jnp.repeat(v_scale.astype(jnp.float32), BLK, axis=0)

    def one_block(item_index):
        block_id = item_index // KVH
        group_id = item_index % KVH
        picked = lax.dynamic_slice(query, (block_id * BLK, group_id * group_size, jnp.int32(0)), (BLK, group_size, DH)).astype(jnp.float32)
        key_rows = lax.dynamic_slice_in_dim(keys, group_id, 1, 1)[:, 0, :].astype(jnp.float32)
        value_rows = lax.dynamic_slice_in_dim(values, group_id, 1, 1)[:, 0, :].astype(jnp.float32)
        key_column = lax.dynamic_slice_in_dim(key_gain, group_id, 1, 1)[:, 0]
        value_column = lax.dynamic_slice_in_dim(value_gain, group_id, 1, 1)[:, 0]
        scores = jnp.einsum('qrd,kd->rqk', picked, key_rows, precision=lax.Precision.HIGHEST)
        scores = scores * (key_column * inv_root)[None, None, :]
        query_place = lax.dynamic_slice_in_dim(token_place, block_id * BLK, BLK)
        visible = query_place[:, None] >= token_place[None, :]
        scores = jnp.where(visible[None], scores, masked_value)
        largest = lax.optimization_barrier(jnp.max(scores, axis=-1, keepdims=True))
        weights = jnp.exp(scores - largest)
        totals = lax.optimization_barrier(jnp.sum(weights, axis=-1))
        rounded = lax.optimization_barrier(weights.astype(jnp.bfloat16)).astype(jnp.float32)
        scaled_values = value_rows * value_column[:, None]
        summed = jnp.einsum('rqk,kd->rqd', rounded, scaled_values, precision=lax.Precision.HIGHEST)
        return (summed / totals[..., None]).astype(jnp.bfloat16)
    blocks = lax.map(one_block, jnp.arange(NBLOCK * KVH, dtype=jnp.int32))
    attended = blocks.reshape(NBLOCK, KVH, group_size, BLK, DH).transpose(0, 3, 1, 2, 4).reshape(TOKENS, HQ * DH)
    slab_width = HEAD_DEV * DH

    def add_group(running, group_index):
        part_rows = lax.dynamic_slice_in_dim(attended, group_index * slab_width, slab_width, 1)
        part_weight = lax.dynamic_slice_in_dim(out_weight, group_index * slab_width, slab_width, 0)
        group_term = jnp.dot(part_rows, part_weight, preferred_element_type=jnp.float32)
        rounded_term = lax.optimization_barrier(group_term.astype(jnp.bfloat16))
        return (running + rounded_term.astype(jnp.float32), None)
    summed_all, unused = lax.scan(add_group, jnp.zeros((TOKENS, D), jnp.float32), jnp.arange(N_HEAD, dtype=jnp.int32))
    return summed_all.astype(jnp.bfloat16)
```

```python
import functools
import math

import jax
import jax.numpy as jnp
from jax import lax
from jax.experimental import pallas as pl
from jax.experimental.pallas import tpu as pltpu
from jax.sharding import PartitionSpec as P

masked_value = -1e30
COLUMN_CHUNKS = 4


def attend_kernel(
    per_group, block_len, head_dim, blocks,
    order, own, key_gain, value_gain,
    q_ref, k_ref, vt_ref, o_ref,
    max_ref, total_ref, sum_ref,
):
    group = pl.program_id(0)
    place = own[pl.program_id(1)]

    def tile(index, first):
        block = order[index]
        owner = lax.div(block, 2)
        start = pl.multiple_of(lax.rem(block, 2) * block_len, block_len)
        key = k_ref[owner, pl.ds(start, block_len), :]
        value_t = vt_ref[owner, :, pl.ds(start, block_len)]
        gain = key_gain[group * blocks + block]
        scale = value_gain[group * blocks + block]
        if first:
            shape = (block_len, block_len)
            visible = lax.broadcasted_iota(jnp.int32, shape, 0) <= lax.broadcasted_iota(
                jnp.int32, shape, 1
            )
        for h in range(per_group):
            columns = slice(h * head_dim, (h + 1) * head_dim)
            scores = lax.dot_general(
                key, q_ref[:, columns], (((1,), (1,)), ((), ())),
                preferred_element_type=jnp.float32,
            )
            if first:
                scores = jnp.where(visible, scores, masked_value)
            top = jnp.max(scores, axis=0, keepdims=True) * gain
            if not first:
                old = max_ref[h : h + 1, :]
                top = jnp.maximum(old, top)
            weights = jnp.exp2(scores * gain - top)
            total = jnp.sum(weights, axis=0, keepdims=True)
            product = lax.dot_general(
                value_t, weights.astype(jnp.bfloat16), (((1,), (0,)), ((), ())),
                preferred_element_type=jnp.float32,
            ) * scale
            if not first:
                factor = jnp.exp2(old - top)
                total = total + factor * total_ref[h : h + 1, :]
                product = product + factor * sum_ref[h]
            max_ref[h : h + 1, :] = top
            total_ref[h : h + 1, :] = total
            sum_ref[h] = product

    tile(place, True)

    @pl.loop(0, place)
    def _(index):
        tile(index, False)

    for h in range(per_group):
        columns = slice(h * head_dim, (h + 1) * head_dim)
        mean = sum_ref[h] / total_ref[h : h + 1, :]
        o_ref[:, columns] = mean.T.astype(o_ref.dtype)


def attend(order, own, key_gain, value_gain, query, keys, values_t, group_count):
    rows, width = query.shape
    devices, _, key_width = keys.shape
    head_dim = key_width // group_count
    slots = own.shape[0]
    block_len = rows // slots
    group_width = width // group_count
    per_group = group_width // head_dim
    blocks = order.shape[0]
    pairs = slots * block_len * rows * devices * per_group * group_count // 2
    return pl.pallas_call(
        functools.partial(attend_kernel, per_group, block_len, head_dim, blocks),
        grid_spec=pltpu.PrefetchScalarGridSpec(
            num_scalar_prefetch=4,
            grid=(group_count, slots),
            in_specs=[
                pl.BlockSpec((block_len, group_width), lambda g, s, *_: (s, g)),
                pl.BlockSpec((devices, rows, head_dim), lambda g, s, *_: (0, 0, g)),
                pl.BlockSpec((devices, head_dim, rows), lambda g, s, *_: (0, g, 0)),
            ],
            out_specs=pl.BlockSpec((block_len, group_width), lambda g, s, *_: (s, g)),
            scratch_shapes=[
                pltpu.VMEM((per_group, block_len), jnp.float32),
                pltpu.VMEM((per_group, block_len), jnp.float32),
                pltpu.VMEM((per_group, head_dim, block_len), jnp.float32),
            ],
        ),
        out_shape=jax.ShapeDtypeStruct((rows, width), jnp.bfloat16),
        compiler_params=pltpu.CompilerParams(vmem_limit_bytes=50 * 1024 * 1024),
        cost_estimate=pl.CostEstimate(
            flops=4 * pairs * head_dim, bytes_accessed=8 << 20, transcendentals=pairs
        ),
    )(order, own, key_gain, value_gain, query, keys, values_t)


def body(query, keys, values, k_scale, v_scale, block_place, out_weight):
    rows, head_count, head_dim = query.shape
    group_count = keys.shape[1]
    slots = block_place.shape[0]
    devices = lax.axis_size("ctx")
    blocks = slots * devices
    width = group_count * head_dim
    facts = jnp.concatenate(
        [k_scale, v_scale, block_place[:, None].astype(jnp.bfloat16)], axis=1
    )
    facts = jnp.pad(facts, ((0, 16 - slots), (0, width - facts.shape[1])))
    key_part = jnp.concatenate([keys.reshape(rows, width), facts], axis=0)
    all_keys = lax.all_gather(key_part, "ctx", axis=0, tiled=False)
    all_values = lax.all_gather(values.reshape(rows, width).T, "ctx", axis=0, tiled=False)
    all_facts = all_keys[:, rows : rows + slots, : 2 * group_count + 1].reshape(blocks, -1)
    all_facts = all_facts.astype(jnp.float32)
    places = all_facts[:, -1].astype(jnp.int32)
    ids = jnp.arange(blocks, dtype=jnp.int32)
    order = jnp.sum(jnp.where(places[None, :] == ids[:, None], ids[None, :], 0), axis=1)
    rate = math.log2(math.e) / math.sqrt(head_dim)
    key_gain = (all_facts[:, :group_count] * rate).T.reshape(-1)
    value_gain = all_facts[:, group_count : 2 * group_count].T.reshape(-1)
    attended = attend(
        order, block_place, key_gain, value_gain,
        query.reshape(rows, head_count * head_dim), all_keys[:, :rows], all_values, group_count,
    )
    step = out_weight.shape[1] // COLUMN_CHUNKS
    pieces = []
    for c in range(COLUMN_CHUNKS):
        term = jnp.dot(
            attended, out_weight[:, c * step : (c + 1) * step],
            preferred_element_type=jnp.float32,
        ).astype(jnp.bfloat16)
        pieces.append(lax.psum_scatter(term, "head", scatter_dimension=0, tiled=True))
    return jnp.concatenate(pieces, axis=1)


def solution(mesh):
    placed = (
        P("ctx", "head", None),
        P("ctx", "head", None),
        P("ctx", "head", None),
        P("ctx", "head"),
        P("ctx", "head"),
        P("ctx"),
        P("head", None),
    )
    return jax.shard_map(
        body, mesh=mesh, in_specs=placed, out_specs=P(("ctx", "head"), None), check_vma=False
    )
```

```python
import functools
import math

import jax
import jax.numpy as jnp
from jax import lax
from jax.experimental import pallas as pl
from jax.experimental.pallas import tpu as pltpu
from jax.sharding import PartitionSpec as P

masked_value = -1e30
COLUMN_STEP = 512
LAG = 3


def attend_kernel(
    per_group, block_len, head_dim, blocks, first_slot, later,
    order, own, key_gain, value_gain,
    q_ref, k_ref, vt_ref, *refs,
):
    group = pl.program_id(0)
    if later:
        old_max, old_total, old_sum, o_ref, max_ref, total_ref, sum_ref = refs
    elif first_slot == 0:
        o_ref, max_ref, total_ref, sum_ref = refs
    else:
        max_ref, total_ref, sum_ref = refs
    place = own[first_slot]

    def tile(index, diagonal, fresh):
        block = order[index]
        owner = lax.div(block, 2)
        key = k_ref[owner]
        value_t = vt_ref[owner]
        gain = key_gain[group * blocks + block]
        scale = value_gain[group * blocks + block]
        if diagonal:
            shape = (block_len, block_len)
            visible = lax.broadcasted_iota(jnp.int32, shape, 0) <= lax.broadcasted_iota(
                jnp.int32, shape, 1
            )
        for h in range(per_group):
            columns = slice(h * head_dim, (h + 1) * head_dim)
            scores = lax.dot_general(
                key, q_ref[:, columns], (((1,), (1,)), ((), ())),
                preferred_element_type=jnp.float32,
            )
            if diagonal:
                scores = jnp.where(visible, scores, masked_value)
            top = jnp.max(scores, axis=0, keepdims=True) * gain
            if not fresh:
                old = max_ref[h : h + 1, :]
                top = jnp.maximum(old, top)
            weights = jnp.exp2(scores * gain - top)
            total = jnp.sum(weights, axis=0, keepdims=True)
            product = lax.dot_general(
                value_t, weights.astype(jnp.bfloat16), (((1,), (0,)), ((), ())),
                preferred_element_type=jnp.float32,
            ) * scale
            if not fresh:
                factor = jnp.exp2(old - top)
                total = total + factor * total_ref[h : h + 1, :]
                product = product + factor * sum_ref[h]
            max_ref[h : h + 1, :] = top
            total_ref[h : h + 1, :] = total
            sum_ref[h] = product

    half = blocks // 2
    if later:
        max_ref[...] = old_max[...]
        total_ref[...] = old_total[...]
        sum_ref[...] = old_sum[...]
        tile(place, True, False)
        start, stop = half, place
    elif first_slot == 0:
        tile(place, True, True)
        start, stop = 0, place
    else:
        tile(0, False, True)
        start, stop = 1, half

    @pl.loop(start, stop)
    def _(index):
        tile(index, False, False)

    if later or first_slot == 0:
        for h in range(per_group):
            columns = slice(h * head_dim, (h + 1) * head_dim)
            mean = sum_ref[h] / total_ref[h : h + 1, :]
            o_ref[:, columns] = mean.T.astype(o_ref.dtype)


def attend(facts, query, gathered, group_count, head_dim, slot, state=None):
    rows, width = query.shape
    devices = gathered.shape[0]
    block_len = rows // 2
    group_width = width // group_count
    per_group = group_width // head_dim
    heads = group_count * per_group
    blocks = facts[0].shape[0]
    later = state is not None
    tiles = blocks // 4 if later or slot == 0 else blocks // 2
    pairs = tiles * block_len * block_len * heads
    row_spec = pl.BlockSpec((per_group, block_len), lambda g, *_: (g, 0))
    sum_spec = pl.BlockSpec((per_group, head_dim, block_len), lambda g, *_: (g, 0, 0))
    state_specs = [row_spec, row_spec, sum_spec]
    row_shape = (per_group, block_len)
    sum_shape = (per_group, head_dim, block_len)
    first_value = block_len // head_dim
    outs = ([pl.BlockSpec((block_len, group_width), lambda g, *_: (0, g))],
            [jax.ShapeDtypeStruct((block_len, width), jnp.bfloat16)])
    scratch = [
        pltpu.VMEM(row_shape, jnp.float32),
        pltpu.VMEM(row_shape, jnp.float32),
        pltpu.VMEM(sum_shape, jnp.float32),
    ]
    if not later and slot == 1:
        outs = (state_specs, [
            jax.ShapeDtypeStruct((heads, block_len), jnp.float32),
            jax.ShapeDtypeStruct((heads, block_len), jnp.float32),
            jax.ShapeDtypeStruct((heads, head_dim, block_len), jnp.float32),
        ])
        scratch = []
    results = pl.pallas_call(
        functools.partial(
            attend_kernel, per_group, block_len, head_dim, blocks, slot, later
        ),
        grid_spec=pltpu.PrefetchScalarGridSpec(
            num_scalar_prefetch=4,
            grid=(group_count,),
            in_specs=[
                pl.BlockSpec((block_len, group_width), lambda g, *_: (slot, g)),
                pl.BlockSpec((devices, block_len, head_dim), lambda g, *_: (0, 0, g)),
                pl.BlockSpec(
                    (devices, head_dim, block_len), lambda g, *_: (0, first_value + g, 0)
                ),
            ] + (state_specs if later else []),
            out_specs=outs[0],
            scratch_shapes=scratch,
        ),
        out_shape=outs[1],
        compiler_params=pltpu.CompilerParams(vmem_limit_bytes=40 * 1024 * 1024),
        cost_estimate=pl.CostEstimate(
            flops=4 * pairs * head_dim, bytes_accessed=4 << 20, transcendentals=pairs
        ),
    )(*facts, query, gathered, gathered, *(state if later else ()))
    return results if len(results) > 1 else results[0]


def project_kernel(
    chunks,
    low_ref, high_ref, w_ref, o_ref,
    lhs, sent, kept, arrived, passed, ended,
    send_one, recv_one, send_two, recv_two,
):
    t = pl.program_id(0)
    me = lax.axis_index("head")
    along_x = me + 1 - 2 * (me % 2)
    along_y = (me + 2) % 4
    part = low_ref.shape[0] // 2

    @pl.when(t == 0)
    def _():
        barrier = pltpu.get_barrier_semaphore()
        for partner in (along_x, along_y):
            pl.semaphore_signal(
                barrier, inc=1, device_id={"head": partner},
                device_id_type=pl.DeviceIdType.MESH,
            )
        for parity in range(2):
            near, far = (along_x, along_y) if parity == 0 else (along_y, along_x)
            for slot, owner in enumerate((3 - me, near, far, me)):
                rows = pl.ds(pl.multiple_of((owner % 2) * part, part), part)

                @pl.when(owner // 2 == 0)
                def _():
                    lhs[parity, slot * part : (slot + 1) * part, :] = low_ref[rows, :]

                @pl.when(owner // 2 == 1)
                def _():
                    lhs[parity, slot * part : (slot + 1) * part, :] = high_ref[rows, :]

        pl.semaphore_wait(barrier, 2)

    def first_copy(c):
        near = along_x + (c % 2) * (along_y - along_x)
        return pltpu.make_async_remote_copy(
            src_ref=sent.at[c], dst_ref=arrived.at[c],
            send_sem=send_one.at[c], recv_sem=recv_one.at[c],
            device_id={"head": near}, device_id_type=pl.DeviceIdType.MESH,
        )

    def second_copy(c):
        far = along_y + (c % 2) * (along_x - along_y)
        return pltpu.make_async_remote_copy(
            src_ref=passed.at[c], dst_ref=ended.at[c],
            send_sem=send_two.at[c], recv_sem=recv_two.at[c],
            device_id={"head": far}, device_id_type=pl.DeviceIdType.MESH,
        )

    @pl.when(t < chunks)
    def _():
        term = jnp.dot(lhs[t % 2], w_ref[...], preferred_element_type=jnp.float32)
        term = term.astype(jnp.bfloat16)
        sent[t] = term[: 2 * part]
        kept[t] = term[2 * part :]
        first_copy(t).start()

    @pl.when((t >= LAG) & (t < chunks + LAG))
    def _():
        c = t - LAG
        first_copy(c).wait()
        passed[c] = (
            arrived[c, :part, :].astype(jnp.float32) + kept[c, :part, :].astype(jnp.float32)
        ).astype(jnp.bfloat16)
        second_copy(c).start()

    @pl.when(t >= 2 * LAG)
    def _():
        c = t - 2 * LAG
        second_copy(c).wait()
        o_ref[...] = (
            arrived[c, part:, :].astype(jnp.float32)
            + kept[c, part:, :].astype(jnp.float32)
            + ended[c].astype(jnp.float32)
        ).astype(jnp.bfloat16)


def project(low, high, weight):
    depth, columns = weight.shape
    rows = 2 * low.shape[0]
    part = rows // 4
    step = COLUMN_STEP
    chunks = columns // step
    last = chunks - 1
    return pl.pallas_call(
        functools.partial(project_kernel, chunks),
        grid_spec=pltpu.PrefetchScalarGridSpec(
            num_scalar_prefetch=0,
            grid=(chunks + 2 * LAG,),
            in_specs=[
                pl.BlockSpec((rows // 2, depth), lambda t: (0, 0)),
                pl.BlockSpec((rows // 2, depth), lambda t: (0, 0)),
                pl.BlockSpec((depth, step), lambda t: (0, jnp.minimum(t, last))),
            ],
            out_specs=pl.BlockSpec((part, step), lambda t: (0, jnp.maximum(t - 2 * LAG, 0))),
            scratch_shapes=[
                pltpu.VMEM((2, rows, depth), jnp.bfloat16),
                pltpu.VMEM((chunks, 2 * part, step), jnp.bfloat16),
                pltpu.VMEM((chunks, 2 * part, step), jnp.bfloat16),
                pltpu.VMEM((chunks, 2 * part, step), jnp.bfloat16),
                pltpu.VMEM((chunks, part, step), jnp.bfloat16),
                pltpu.VMEM((chunks, part, step), jnp.bfloat16),
                pltpu.SemaphoreType.DMA((chunks,)),
                pltpu.SemaphoreType.DMA((chunks,)),
                pltpu.SemaphoreType.DMA((chunks,)),
                pltpu.SemaphoreType.DMA((chunks,)),
            ],
        ),
        out_shape=jax.ShapeDtypeStruct((part, columns), jnp.bfloat16),
        compiler_params=pltpu.CompilerParams(
            collective_id=0, has_side_effects=True, vmem_limit_bytes=56 * 1024 * 1024
        ),
        cost_estimate=pl.CostEstimate(
            flops=2 * rows * depth * columns, bytes_accessed=2 * depth * columns,
            transcendentals=0,
        ),
    )(low, high, weight)


def body(query, keys, values, k_scale, v_scale, block_place, out_weight):
    rows, head_count, head_dim = query.shape
    group_count = keys.shape[1]
    slots = block_place.shape[0]
    devices = lax.axis_size("ctx")
    blocks = slots * devices
    block_len = rows // slots
    width = group_count * head_dim
    facts = jnp.concatenate(
        [k_scale, v_scale, block_place[:, None].astype(jnp.bfloat16)], axis=1
    )
    facts = jnp.pad(facts, ((0, 16 - slots), (0, block_len - facts.shape[1])))

    def payload(slot):
        part = slice(slot * block_len, (slot + 1) * block_len)
        key = keys[part].reshape(block_len, width)
        key = jnp.pad(key, ((0, 0), (0, block_len - width))) if width < block_len else key
        return [key, values[part].reshape(block_len, width).T]

    low_part = lax.all_gather(jnp.concatenate(payload(0) + [facts]), "ctx", axis=0)
    high_part = lax.all_gather(jnp.concatenate(payload(1)), "ctx", axis=0)
    base = block_len + width
    all_facts = low_part[:, base : base + slots, : 2 * group_count + 1].reshape(blocks, -1)
    all_facts = all_facts.astype(jnp.float32)
    places = all_facts[:, -1].astype(jnp.int32)
    ids = jnp.arange(blocks, dtype=jnp.int32)
    order = jnp.sum(jnp.where(places[None, :] == ids[:, None], ids[None, :], 0), axis=1)
    rate = math.log2(math.e) / math.sqrt(head_dim)
    key_gain = (all_facts[:, :group_count] * rate).T.reshape(-1)
    value_gain = all_facts[:, group_count : 2 * group_count].T.reshape(-1)
    known = (order, block_place, key_gain, value_gain)
    flat = query.reshape(rows, head_count * head_dim)
    state = attend(known, flat, low_part, group_count, head_dim, 1)
    low = attend(known, flat, low_part, group_count, head_dim, 0)
    high = attend(known, flat, high_part, group_count, head_dim, 1, state)
    if lax.axis_size("head") == 4:
        return project(low, high, out_weight)
    term = jnp.dot(jnp.concatenate([low, high]), out_weight, preferred_element_type=jnp.float32)
    return lax.psum_scatter(
        term.astype(jnp.bfloat16), "head", scatter_dimension=0, tiled=True
    )


def solution(mesh):
    placed = (
        P("ctx", "head", None),
        P("ctx", "head", None),
        P("ctx", "head", None),
        P("ctx", "head"),
        P("ctx", "head"),
        P("ctx"),
        P("head", None),
    )
    return jax.shard_map(
        body, mesh=mesh, in_specs=placed, out_specs=P(("ctx", "head"), None), check_vma=False
    )
```

```python
import functools
import math

import jax
import jax.numpy as jnp
from jax import lax
from jax.experimental import pallas as pl
from jax.experimental.pallas import tpu as pltpu
from jax.sharding import PartitionSpec as P

masked_value = -1e30
COLUMN_STEP = 512
LAG = 3


def attend_kernel(
    per_group, block_len, head_dim, blocks, first_slot, later,
    order, own, key_gain, value_gain,
    q_ref, k_ref, vt_ref, *refs,
):
    group = pl.program_id(0)
    query_ref = refs[-1]
    if later:
        old_max, old_total, old_sum, o_ref, max_ref, total_ref, sum_ref = refs[:-1]
    elif first_slot == 0:
        o_ref, max_ref, total_ref, sum_ref = refs[:-1]
    else:
        max_ref, total_ref, sum_ref = refs[:-1]
    place = own[first_slot]
    for h in range(per_group):
        query_ref[h] = q_ref[:, h * head_dim : (h + 1) * head_dim].T

    def visit(indices, diagonal):
        found = [order[index] for index in indices]
        keys = [k_ref[lax.div(block, 2)] for block in found]
        values = [vt_ref[lax.div(block, 2)] for block in found]
        gains = [key_gain[group * blocks + block] for block in found]
        scales = [value_gain[group * blocks + block] for block in found]
        if diagonal:
            shape = (block_len, block_len)
            visible = lax.broadcasted_iota(jnp.int32, shape, 0) <= lax.broadcasted_iota(
                jnp.int32, shape, 1
            )

        def score(h):
            result = [
                jnp.dot(key, query_ref[h], preferred_element_type=jnp.float32) for key in keys
            ]
            if diagonal:
                result[-1] = jnp.where(visible, result[-1], masked_value)
            return result

        def weigh(h, scores):
            old = max_ref[h : h + 1, :]
            top = old
            for part, gain in zip(scores, gains):
                top = jnp.maximum(top, jnp.max(part, axis=0, keepdims=True) * gain)
            factor = jnp.exp2(old - top)
            total = factor * total_ref[h : h + 1, :]
            rounded = []
            for part, gain in zip(scores, gains):
                weights = jnp.exp2(part * gain - top)
                total = total + jnp.sum(weights, axis=0, keepdims=True)
                rounded.append(weights.astype(jnp.bfloat16))
            max_ref[h : h + 1, :] = top
            total_ref[h : h + 1, :] = total
            return rounded, factor

        def gather(h, rounded, factor):
            running = factor * sum_ref[h]
            for part, value, scale in zip(rounded, values, scales):
                running = running + scale * jnp.dot(
                    value, part, preferred_element_type=jnp.float32
                )
            sum_ref[h] = running

        scores = score(0)
        waiting = None
        for h in range(per_group):
            upcoming = score(h + 1) if h + 1 < per_group else None
            if waiting is not None:
                gather(h - 1, *waiting)
            waiting = weigh(h, scores)
            scores = upcoming
        gather(per_group - 1, *waiting)

    half = blocks // 2
    if later:
        max_ref[...] = old_max[...]
        total_ref[...] = old_total[...]
        sum_ref[...] = old_sum[...]
        start, stop = half, place
    else:
        max_ref[...] = jnp.full(max_ref.shape, masked_value, jnp.float32)
        total_ref[...] = jnp.zeros(total_ref.shape, jnp.float32)
        sum_ref[...] = jnp.zeros(sum_ref.shape, jnp.float32)
        start, stop = 0, (place if first_slot == 0 else half)
    pairs = (stop - start) // 2

    @pl.loop(0, pairs)
    def _(pair):
        visit([start + 2 * pair, start + 2 * pair + 1], False)

    if later or first_slot == 0:
        odd = (stop - start) - 2 * pairs

        @pl.when(odd == 1)
        def _():
            visit([place - 1, place], True)

        @pl.when(odd == 0)
        def _():
            visit([place], True)

        for h in range(per_group):
            columns = slice(h * head_dim, (h + 1) * head_dim)
            mean = sum_ref[h] / total_ref[h : h + 1, :]
            o_ref[:, columns] = mean.T.astype(o_ref.dtype)
    elif half % 2:
        visit([half - 1], False)


def attend(facts, query, gathered, group_count, head_dim, slot, state=None):
    rows, width = query.shape
    devices = gathered.shape[0]
    block_len = rows // 2
    group_width = width // group_count
    per_group = group_width // head_dim
    heads = group_count * per_group
    blocks = facts[0].shape[0]
    later = state is not None
    tiles = blocks // 4 if later or slot == 0 else blocks // 2
    pairs = tiles * block_len * block_len * heads
    row_spec = pl.BlockSpec((per_group, block_len), lambda g, *_: (g, 0))
    sum_spec = pl.BlockSpec((per_group, head_dim, block_len), lambda g, *_: (g, 0, 0))
    state_specs = [row_spec, row_spec, sum_spec]
    row_shape = (per_group, block_len)
    sum_shape = (per_group, head_dim, block_len)
    first_value = block_len // head_dim
    outs = ([pl.BlockSpec((block_len, group_width), lambda g, *_: (0, g))],
            [jax.ShapeDtypeStruct((block_len, width), jnp.bfloat16)])
    scratch = [
        pltpu.VMEM(row_shape, jnp.float32),
        pltpu.VMEM(row_shape, jnp.float32),
        pltpu.VMEM(sum_shape, jnp.float32),
    ]
    if not later and slot == 1:
        outs = (state_specs, [
            jax.ShapeDtypeStruct((heads, block_len), jnp.float32),
            jax.ShapeDtypeStruct((heads, block_len), jnp.float32),
            jax.ShapeDtypeStruct((heads, head_dim, block_len), jnp.float32),
        ])
        scratch = []
    scratch.append(pltpu.VMEM((per_group, head_dim, block_len), jnp.bfloat16))
    results = pl.pallas_call(
        functools.partial(
            attend_kernel, per_group, block_len, head_dim, blocks, slot, later
        ),
        grid_spec=pltpu.PrefetchScalarGridSpec(
            num_scalar_prefetch=4,
            grid=(group_count,),
            in_specs=[
                pl.BlockSpec((block_len, group_width), lambda g, *_: (slot, g)),
                pl.BlockSpec((devices, block_len, head_dim), lambda g, *_: (0, 0, g)),
                pl.BlockSpec(
                    (devices, head_dim, block_len), lambda g, *_: (0, first_value + g, 0)
                ),
            ] + (state_specs if later else []),
            out_specs=outs[0],
            scratch_shapes=scratch,
        ),
        out_shape=outs[1],
        compiler_params=pltpu.CompilerParams(vmem_limit_bytes=40 * 1024 * 1024),
        cost_estimate=pl.CostEstimate(
            flops=4 * pairs * head_dim, bytes_accessed=4 << 20, transcendentals=pairs
        ),
    )(*facts, query, gathered, gathered, *(state if later else ()))
    return results if len(results) > 1 else results[0]


def project_kernel(
    chunks,
    low_ref, high_ref, w_ref, o_ref,
    lhs, sent, kept, arrived, passed, ended,
    send_one, recv_one, send_two, recv_two,
):
    t = pl.program_id(0)
    me = lax.axis_index("head")
    along_x = me + 1 - 2 * (me % 2)
    along_y = (me + 2) % 4
    part = low_ref.shape[0] // 2

    @pl.when(t == 0)
    def _():
        barrier = pltpu.get_barrier_semaphore()
        for partner in (along_x, along_y):
            pl.semaphore_signal(
                barrier, inc=1, device_id={"head": partner},
                device_id_type=pl.DeviceIdType.MESH,
            )
        for parity in range(2):
            near, far = (along_x, along_y) if parity == 0 else (along_y, along_x)
            for slot, owner in enumerate((3 - me, near, far, me)):
                rows = pl.ds(pl.multiple_of((owner % 2) * part, part), part)

                @pl.when(owner // 2 == 0)
                def _():
                    lhs[parity, slot * part : (slot + 1) * part, :] = low_ref[rows, :]

                @pl.when(owner // 2 == 1)
                def _():
                    lhs[parity, slot * part : (slot + 1) * part, :] = high_ref[rows, :]

        pl.semaphore_wait(barrier, 2)

    def first_copy(c):
        near = along_x + (c % 2) * (along_y - along_x)
        return pltpu.make_async_remote_copy(
            src_ref=sent.at[c], dst_ref=arrived.at[c],
            send_sem=send_one.at[c], recv_sem=recv_one.at[c],
            device_id={"head": near}, device_id_type=pl.DeviceIdType.MESH,
        )

    def second_copy(c):
        far = along_y + (c % 2) * (along_x - along_y)
        return pltpu.make_async_remote_copy(
            src_ref=passed.at[c], dst_ref=ended.at[c],
            send_sem=send_two.at[c], recv_sem=recv_two.at[c],
            device_id={"head": far}, device_id_type=pl.DeviceIdType.MESH,
        )

    @pl.when(t < chunks)
    def _():
        term = jnp.dot(lhs[t % 2], w_ref[...], preferred_element_type=jnp.float32)
        term = term.astype(jnp.bfloat16)
        sent[t] = term[: 2 * part]
        kept[t] = term[2 * part :]
        first_copy(t).start()

    @pl.when((t >= LAG) & (t < chunks + LAG))
    def _():
        c = t - LAG
        first_copy(c).wait()
        passed[c] = (
            arrived[c, :part, :].astype(jnp.float32) + kept[c, :part, :].astype(jnp.float32)
        ).astype(jnp.bfloat16)
        second_copy(c).start()

    @pl.when(t >= 2 * LAG)
    def _():
        c = t - 2 * LAG
        second_copy(c).wait()
        o_ref[...] = (
            arrived[c, part:, :].astype(jnp.float32)
            + kept[c, part:, :].astype(jnp.float32)
            + ended[c].astype(jnp.float32)
        ).astype(jnp.bfloat16)


def project(low, high, weight):
    depth, columns = weight.shape
    rows = 2 * low.shape[0]
    part = rows // 4
    step = COLUMN_STEP
    chunks = columns // step
    last = chunks - 1
    return pl.pallas_call(
        functools.partial(project_kernel, chunks),
        grid_spec=pltpu.PrefetchScalarGridSpec(
            num_scalar_prefetch=0,
            grid=(chunks + 2 * LAG,),
            in_specs=[
                pl.BlockSpec((rows // 2, depth), lambda t: (0, 0)),
                pl.BlockSpec((rows // 2, depth), lambda t: (0, 0)),
                pl.BlockSpec((depth, step), lambda t: (0, jnp.minimum(t, last))),
            ],
            out_specs=pl.BlockSpec((part, step), lambda t: (0, jnp.maximum(t - 2 * LAG, 0))),
            scratch_shapes=[
                pltpu.VMEM((2, rows, depth), jnp.bfloat16),
                pltpu.VMEM((chunks, 2 * part, step), jnp.bfloat16),
                pltpu.VMEM((chunks, 2 * part, step), jnp.bfloat16),
                pltpu.VMEM((chunks, 2 * part, step), jnp.bfloat16),
                pltpu.VMEM((chunks, part, step), jnp.bfloat16),
                pltpu.VMEM((chunks, part, step), jnp.bfloat16),
                pltpu.SemaphoreType.DMA((chunks,)),
                pltpu.SemaphoreType.DMA((chunks,)),
                pltpu.SemaphoreType.DMA((chunks,)),
                pltpu.SemaphoreType.DMA((chunks,)),
            ],
        ),
        out_shape=jax.ShapeDtypeStruct((part, columns), jnp.bfloat16),
        compiler_params=pltpu.CompilerParams(
            collective_id=0, has_side_effects=True, vmem_limit_bytes=56 * 1024 * 1024
        ),
        cost_estimate=pl.CostEstimate(
            flops=2 * rows * depth * columns, bytes_accessed=2 * depth * columns,
            transcendentals=0,
        ),
    )(low, high, weight)


def body(query, keys, values, k_scale, v_scale, block_place, out_weight):
    rows, head_count, head_dim = query.shape
    group_count = keys.shape[1]
    slots = block_place.shape[0]
    devices = lax.axis_size("ctx")
    blocks = slots * devices
    block_len = rows // slots
    width = group_count * head_dim
    facts = jnp.concatenate(
        [k_scale, v_scale, block_place[:, None].astype(jnp.bfloat16)], axis=1
    )
    facts = jnp.pad(facts, ((0, 16 - slots), (0, block_len - facts.shape[1])))

    def payload(slot):
        part = slice(slot * block_len, (slot + 1) * block_len)
        key = keys[part].reshape(block_len, width)
        key = jnp.pad(key, ((0, 0), (0, block_len - width))) if width < block_len else key
        return [key, values[part].reshape(block_len, width).T]

    low_part = lax.all_gather(jnp.concatenate(payload(0) + [facts]), "ctx", axis=0)
    high_part = lax.all_gather(jnp.concatenate(payload(1)), "ctx", axis=0)
    base = block_len + width
    all_facts = low_part[:, base : base + slots, : 2 * group_count + 1].reshape(blocks, -1)
    all_facts = all_facts.astype(jnp.float32)
    places = all_facts[:, -1].astype(jnp.int32)
    ids = jnp.arange(blocks, dtype=jnp.int32)
    order = jnp.sum(jnp.where(places[None, :] == ids[:, None], ids[None, :], 0), axis=1)
    rate = math.log2(math.e) / math.sqrt(head_dim)
    key_gain = (all_facts[:, :group_count] * rate).T.reshape(-1)
    value_gain = all_facts[:, group_count : 2 * group_count].T.reshape(-1)
    known = (order, block_place, key_gain, value_gain)
    flat = query.reshape(rows, head_count * head_dim)
    state = attend(known, flat, low_part, group_count, head_dim, 1)
    low = attend(known, flat, low_part, group_count, head_dim, 0)
    high = attend(known, flat, high_part, group_count, head_dim, 1, state)
    if lax.axis_size("head") == 4:
        return project(low, high, out_weight)
    term = jnp.dot(jnp.concatenate([low, high]), out_weight, preferred_element_type=jnp.float32)
    return lax.psum_scatter(
        term.astype(jnp.bfloat16), "head", scatter_dimension=0, tiled=True
    )


def solution(mesh):
    placed = (
        P("ctx", "head", None),
        P("ctx", "head", None),
        P("ctx", "head", None),
        P("ctx", "head"),
        P("ctx", "head"),
        P("ctx"),
        P("head", None),
    )
    return jax.shard_map(
        body, mesh=mesh, in_specs=placed, out_specs=P(("ctx", "head"), None), check_vma=False
    )
```

```python
import functools
import math

import jax
import jax.numpy as jnp
from jax import lax
from jax.experimental import pallas as pl
from jax.experimental.pallas import tpu as pltpu
from jax.sharding import PartitionSpec as P

masked_value = -1e30
COLUMN_STEP = 256
LAG = 4


def attend_kernel(
    per_group, block_len, head_dim, blocks, first_slot, later,
    order, own, key_gain, value_gain,
    q_ref, k_ref, vt_ref, *refs,
):
    group = pl.program_id(0)
    query_ref = refs[-1]
    if later:
        old_max, old_total, old_sum, o_ref, max_ref, total_ref, sum_ref = refs[:-1]
    elif first_slot == 0:
        o_ref, max_ref, total_ref, sum_ref = refs[:-1]
    else:
        max_ref, total_ref, sum_ref = refs[:-1]
    place = own[first_slot]
    for h in range(per_group):
        query_ref[h] = q_ref[:, h * head_dim : (h + 1) * head_dim].T

    def visit(indices, diagonal):
        found = [order[index] for index in indices]
        keys = [k_ref[lax.div(block, 2)] for block in found]
        values = [vt_ref[lax.div(block, 2)] for block in found]
        gains = [key_gain[group * blocks + block] for block in found]
        scales = [value_gain[group * blocks + block] for block in found]
        if diagonal:
            shape = (block_len, block_len)
            visible = lax.broadcasted_iota(jnp.int32, shape, 0) <= lax.broadcasted_iota(
                jnp.int32, shape, 1
            )

        def score(h):
            result = [
                jnp.dot(key, query_ref[h], preferred_element_type=jnp.float32) for key in keys
            ]
            if diagonal:
                result[-1] = jnp.where(visible, result[-1], masked_value)
            return result

        def weigh(h, scores):
            old = max_ref[h : h + 1, :]
            top = old
            for part, gain in zip(scores, gains):
                top = jnp.maximum(top, jnp.max(part, axis=0, keepdims=True) * gain)
            factor = jnp.exp2(old - top)
            total = factor * total_ref[h : h + 1, :]
            rounded = []
            for part, gain in zip(scores, gains):
                weights = jnp.exp2(part * gain - top)
                total = total + jnp.sum(weights, axis=0, keepdims=True)
                rounded.append(weights.astype(jnp.bfloat16))
            max_ref[h : h + 1, :] = top
            total_ref[h : h + 1, :] = total
            return rounded, factor

        def gather(h, rounded, factor):
            running = factor * sum_ref[h]
            for part, value, scale in zip(rounded, values, scales):
                running = running + scale * jnp.dot(
                    value, part, preferred_element_type=jnp.float32
                )
            sum_ref[h] = running

        scores = score(0)
        waiting = None
        for h in range(per_group):
            upcoming = score(h + 1) if h + 1 < per_group else None
            if waiting is not None:
                gather(h - 1, *waiting)
            waiting = weigh(h, scores)
            scores = upcoming
        gather(per_group - 1, *waiting)

    half = blocks // 2
    if later:
        max_ref[...] = old_max[...]
        total_ref[...] = old_total[...]
        sum_ref[...] = old_sum[...]
        start, stop = half, place
    else:
        max_ref[...] = jnp.full(max_ref.shape, masked_value, jnp.float32)
        total_ref[...] = jnp.zeros(total_ref.shape, jnp.float32)
        sum_ref[...] = jnp.zeros(sum_ref.shape, jnp.float32)
        start, stop = 0, (place if first_slot == 0 else half)
    pairs = (stop - start) // 2

    @pl.loop(0, pairs)
    def _(pair):
        visit([start + 2 * pair, start + 2 * pair + 1], False)

    if later or first_slot == 0:
        odd = (stop - start) - 2 * pairs

        @pl.when(odd == 1)
        def _():
            visit([place - 1, place], True)

        @pl.when(odd == 0)
        def _():
            visit([place], True)

        for h in range(per_group):
            columns = slice(h * head_dim, (h + 1) * head_dim)
            mean = sum_ref[h] / total_ref[h : h + 1, :]
            o_ref[:, columns] = mean.T.astype(o_ref.dtype)
    elif half % 2:
        visit([half - 1], False)


def attend(facts, query, gathered, group_count, head_dim, slot, state=None):
    rows, width = query.shape
    devices = gathered.shape[0]
    block_len = rows // 2
    group_width = width // group_count
    per_group = group_width // head_dim
    heads = group_count * per_group
    blocks = facts[0].shape[0]
    later = state is not None
    tiles = blocks // 4 if later or slot == 0 else blocks // 2
    pairs = tiles * block_len * block_len * heads
    row_spec = pl.BlockSpec((per_group, block_len), lambda g, *_: (g, 0))
    sum_spec = pl.BlockSpec((per_group, head_dim, block_len), lambda g, *_: (g, 0, 0))
    state_specs = [row_spec, row_spec, sum_spec]
    row_shape = (per_group, block_len)
    sum_shape = (per_group, head_dim, block_len)
    first_value = block_len // head_dim
    outs = ([pl.BlockSpec((block_len, group_width), lambda g, *_: (0, g))],
            [jax.ShapeDtypeStruct((block_len, width), jnp.bfloat16)])
    scratch = [
        pltpu.VMEM(row_shape, jnp.float32),
        pltpu.VMEM(row_shape, jnp.float32),
        pltpu.VMEM(sum_shape, jnp.float32),
    ]
    if not later and slot == 1:
        outs = (state_specs, [
            jax.ShapeDtypeStruct((heads, block_len), jnp.float32),
            jax.ShapeDtypeStruct((heads, block_len), jnp.float32),
            jax.ShapeDtypeStruct((heads, head_dim, block_len), jnp.float32),
        ])
        scratch = []
    scratch.append(pltpu.VMEM((per_group, head_dim, block_len), jnp.bfloat16))
    results = pl.pallas_call(
        functools.partial(
            attend_kernel, per_group, block_len, head_dim, blocks, slot, later
        ),
        grid_spec=pltpu.PrefetchScalarGridSpec(
            num_scalar_prefetch=4,
            grid=(group_count,),
            in_specs=[
                pl.BlockSpec((block_len, group_width), lambda g, *_: (slot, g)),
                pl.BlockSpec((devices, block_len, head_dim), lambda g, *_: (0, 0, g)),
                pl.BlockSpec(
                    (devices, head_dim, block_len), lambda g, *_: (0, first_value + g, 0)
                ),
            ] + (state_specs if later else []),
            out_specs=outs[0],
            scratch_shapes=scratch,
        ),
        out_shape=outs[1],
        compiler_params=pltpu.CompilerParams(vmem_limit_bytes=40 * 1024 * 1024),
        cost_estimate=pl.CostEstimate(
            flops=4 * pairs * head_dim, bytes_accessed=4 << 20, transcendentals=pairs
        ),
    )(*facts, query, gathered, gathered, *(state if later else ()))
    return results if len(results) > 1 else results[0]


def project_kernel(
    chunks,
    low_ref, high_ref, w_ref, o_ref,
    lhs, sent, kept, arrived, passed, ended,
    send_one, recv_one, send_two, recv_two,
):
    t = pl.program_id(0)
    me = lax.axis_index("head")
    along_x = me + 1 - 2 * (me % 2)
    along_y = (me + 2) % 4
    part = low_ref.shape[0] // 2

    @pl.when(t == 0)
    def _():
        barrier = pltpu.get_barrier_semaphore()
        for partner in (along_x, along_y):
            pl.semaphore_signal(
                barrier, inc=1, device_id={"head": partner},
                device_id_type=pl.DeviceIdType.MESH,
            )
        for parity in range(2):
            near, far = (along_x, along_y) if parity == 0 else (along_y, along_x)
            for slot, owner in enumerate((3 - me, near, far, me)):
                rows = pl.ds(pl.multiple_of((owner % 2) * part, part), part)

                @pl.when(owner // 2 == 0)
                def _():
                    lhs[parity, slot * part : (slot + 1) * part, :] = low_ref[rows, :]

                @pl.when(owner // 2 == 1)
                def _():
                    lhs[parity, slot * part : (slot + 1) * part, :] = high_ref[rows, :]

        pl.semaphore_wait(barrier, 2)

    def first_copy(c):
        near = along_x + (c % 2) * (along_y - along_x)
        return pltpu.make_async_remote_copy(
            src_ref=sent.at[c], dst_ref=arrived.at[c],
            send_sem=send_one.at[c], recv_sem=recv_one.at[c],
            device_id={"head": near}, device_id_type=pl.DeviceIdType.MESH,
        )

    def second_copy(c):
        far = along_y + (c % 2) * (along_x - along_y)
        return pltpu.make_async_remote_copy(
            src_ref=passed.at[c], dst_ref=ended.at[c],
            send_sem=send_two.at[c], recv_sem=recv_two.at[c],
            device_id={"head": far}, device_id_type=pl.DeviceIdType.MESH,
        )

    @pl.when(t < chunks)
    def _():
        term = jnp.dot(lhs[t % 2], w_ref[...], preferred_element_type=jnp.float32)
        term = term.astype(jnp.bfloat16)
        sent[t] = term[: 2 * part]
        kept[t] = term[2 * part :]
        first_copy(t).start()

    @pl.when((t >= LAG) & (t < chunks + LAG))
    def _():
        c = t - LAG
        first_copy(c).wait()
        passed[c] = (
            arrived[c, :part, :].astype(jnp.float32) + kept[c, :part, :].astype(jnp.float32)
        ).astype(jnp.bfloat16)
        second_copy(c).start()

    @pl.when(t >= 2 * LAG)
    def _():
        c = t - 2 * LAG
        second_copy(c).wait()
        o_ref[...] = (
            arrived[c, part:, :].astype(jnp.float32)
            + kept[c, part:, :].astype(jnp.float32)
            + ended[c].astype(jnp.float32)
        ).astype(jnp.bfloat16)


def project(low, high, weight):
    depth, columns = weight.shape
    rows = 2 * low.shape[0]
    part = rows // 4
    step = COLUMN_STEP
    chunks = columns // step
    last = chunks - 1
    return pl.pallas_call(
        functools.partial(project_kernel, chunks),
        grid_spec=pltpu.PrefetchScalarGridSpec(
            num_scalar_prefetch=0,
            grid=(chunks + 2 * LAG,),
            in_specs=[
                pl.BlockSpec((rows // 2, depth), lambda t: (0, 0)),
                pl.BlockSpec((rows // 2, depth), lambda t: (0, 0)),
                pl.BlockSpec((depth, step), lambda t: (0, jnp.minimum(t, last))),
            ],
            out_specs=pl.BlockSpec((part, step), lambda t: (0, jnp.maximum(t - 2 * LAG, 0))),
            scratch_shapes=[
                pltpu.VMEM((2, rows, depth), jnp.bfloat16),
                pltpu.VMEM((chunks, 2 * part, step), jnp.bfloat16),
                pltpu.VMEM((chunks, 2 * part, step), jnp.bfloat16),
                pltpu.VMEM((chunks, 2 * part, step), jnp.bfloat16),
                pltpu.VMEM((chunks, part, step), jnp.bfloat16),
                pltpu.VMEM((chunks, part, step), jnp.bfloat16),
                pltpu.SemaphoreType.DMA((chunks,)),
                pltpu.SemaphoreType.DMA((chunks,)),
                pltpu.SemaphoreType.DMA((chunks,)),
                pltpu.SemaphoreType.DMA((chunks,)),
            ],
        ),
        out_shape=jax.ShapeDtypeStruct((part, columns), jnp.bfloat16),
        compiler_params=pltpu.CompilerParams(
            collective_id=0, has_side_effects=True, vmem_limit_bytes=56 * 1024 * 1024
        ),
        cost_estimate=pl.CostEstimate(
            flops=2 * rows * depth * columns, bytes_accessed=2 * depth * columns,
            transcendentals=0,
        ),
    )(low, high, weight)


def body(query, keys, values, k_scale, v_scale, block_place, out_weight):
    rows, head_count, head_dim = query.shape
    group_count = keys.shape[1]
    slots = block_place.shape[0]
    devices = lax.axis_size("ctx")
    blocks = slots * devices
    block_len = rows // slots
    width = group_count * head_dim
    facts = jnp.concatenate(
        [k_scale, v_scale, block_place[:, None].astype(jnp.bfloat16)], axis=1
    )
    facts = jnp.pad(facts, ((0, 16 - slots), (0, block_len - facts.shape[1])))

    def payload(slot):
        part = slice(slot * block_len, (slot + 1) * block_len)
        key = keys[part].reshape(block_len, width)
        key = jnp.pad(key, ((0, 0), (0, block_len - width))) if width < block_len else key
        return [key, values[part].reshape(block_len, width).T]

    low_part = lax.all_gather(jnp.concatenate(payload(0) + [facts]), "ctx", axis=0)
    high_part = lax.all_gather(jnp.concatenate(payload(1)), "ctx", axis=0)
    base = block_len + width
    all_facts = low_part[:, base : base + slots, : 2 * group_count + 1].reshape(blocks, -1)
    all_facts = all_facts.astype(jnp.float32)
    places = all_facts[:, -1].astype(jnp.int32)
    ids = jnp.arange(blocks, dtype=jnp.int32)
    order = jnp.sum(jnp.where(places[None, :] == ids[:, None], ids[None, :], 0), axis=1)
    rate = math.log2(math.e) / math.sqrt(head_dim)
    key_gain = (all_facts[:, :group_count] * rate).T.reshape(-1)
    value_gain = all_facts[:, group_count : 2 * group_count].T.reshape(-1)
    known = (order, block_place, key_gain, value_gain)
    flat = query.reshape(rows, head_count * head_dim)
    state = attend(known, flat, low_part, group_count, head_dim, 1)
    low = attend(known, flat, low_part, group_count, head_dim, 0)
    high = attend(known, flat, high_part, group_count, head_dim, 1, state)
    if lax.axis_size("head") == 4:
        return project(low, high, out_weight)
    term = jnp.dot(jnp.concatenate([low, high]), out_weight, preferred_element_type=jnp.float32)
    return lax.psum_scatter(
        term.astype(jnp.bfloat16), "head", scatter_dimension=0, tiled=True
    )


def solution(mesh):
    placed = (
        P("ctx", "head", None),
        P("ctx", "head", None),
        P("ctx", "head", None),
        P("ctx", "head"),
        P("ctx", "head"),
        P("ctx"),
        P("head", None),
    )
    return jax.shard_map(
        body, mesh=mesh, in_specs=placed, out_specs=P(("ctx", "head"), None), check_vma=False
    )
```
